128 devices in a mesh: row: 16 (over y, x), col: 8 (over z, core).
Axes of the slice: x: 4, y: 4, z: 4, core: 2. Of those that a mesh axis runs over, the one named last changes fastest.
Arguments:
- panel: float32 [32768, 256], P('row', 'col'), may hold values from -60 to 60
- trailing_in: float32 [32768, 10240], P('row', 'col'), may hold values from -60 to 60
Outputs:
- r_factor: float32 [256, 256], replicated
- q_panel: float32 [32768, 256], P('row')
- r_trail: float32 [256, 10240], P(None, 'col')
- trailing_out: float32 [32768, 10240], P('row', 'col')
The draws below stay inside these ranges and needn't reach their ends.
All inputs are finite; a program needn't handle non-finite values.
Results may differ from the reference program's by a relative error of at most 0.00012.
Values sent between devices are 32-bit elements; how exact they have to be, the bound alone decides.
A program may use at most 128 MiB of HBM per device.

```python
import math
import jax
import jax.numpy as jnp
from jax import lax

B = 256
ROWS = 32768
TRAIL = 10240


def row_factor(subkey, count_rows):
    position = jnp.arange(count_rows, dtype=jnp.float32)
    ramp_factor = jnp.exp(0.55 * position / count_rows)
    spread = jnp.exp(jax.random.uniform(subkey, (count_rows,), jnp.float32, math.log(0.4), math.log(4.0)))
    return ramp_factor * spread


def rough_rows(subkeys, columns):
    base_rows = jax.random.normal(subkeys[0], (ROWS, columns), jnp.float32)
    return base_rows


def draw_panel(key, part):
    subkeys = jax.random.split(jax.random.fold_in(key, 17), 5)
    base_rows = rough_rows(subkeys, B)
    mixing = jnp.eye(B, dtype=jnp.float32) + 0.4 / math.sqrt(B) * jax.random.normal(subkeys[1], (B, B), jnp.float32)
    mixed_rows = jnp.dot(base_rows, mixing, precision=lax.Precision.HIGHEST)
    return jnp.clip(mixed_rows * row_factor(subkeys[2], ROWS)[:, None], -60.0, 60.0)


def draw_trailing_in(key, part):
    subkeys = jax.random.split(jax.random.fold_in(key, 29), 5)
    base_rows = rough_rows(subkeys, TRAIL)
    return jnp.clip(base_rows * row_factor(subkeys[2], ROWS)[:, None], -60.0, 60.0)


def setup_inputs(seed: int = 0) -> dict:
    key_of = jax.random.split(jax.random.key(seed), 3)
    panel = draw_panel(jax.random.fold_in(key_of[2], 71), 0)
    trailing_in = draw_trailing_in(jax.random.fold_in(key_of[2], 71), 0)
    return dict(panel=panel, trailing_in=trailing_in)


def reference(panel, trailing_in):
    highest = lax.Precision.HIGHEST
    gram = jnp.dot(panel.T, panel, precision=highest) / ROWS
    lower_factor = jnp.linalg.cholesky(gram)
    identity = jnp.eye(B, dtype=panel.dtype)
    l_inverse = jax.scipy.linalg.solve_triangular(lower_factor, identity, lower=True)
    q_panel = jnp.dot(panel, l_inverse.T, precision=highest)
    inv_root = 1.0 / math.sqrt(ROWS)
    r_trail = jnp.dot(q_panel.T, trailing_in, precision=highest) * inv_root
    trailing_out = trailing_in - jnp.dot(q_panel, r_trail, precision=highest) * inv_root
    return (lower_factor.T, q_panel, r_trail, trailing_out)
```

```python
import functools
import math

import jax
import jax.numpy as jnp
from jax import lax
from jax.experimental import pallas as pl
from jax.experimental.pallas import tpu as pltpu
from jax.sharding import PartitionSpec as P

F32 = jnp.float32
BF16 = jnp.bfloat16
NN = (((1,), (0,)), ((), ()))
NT = (((1,), (1,)), ((), ()))
TN = (((0,), (0,)), ((), ()))
BLOCK = 32
TILE = 256
dot = functools.partial(lax.dot_general, preferred_element_type=F32)


def split2(x):
    high = x.astype(BF16)
    return high, (x - high.astype(F32)).astype(BF16)


def split3(x):
    high = x.astype(BF16)
    rest = x - high.astype(F32)
    middle = rest.astype(BF16)
    return high, middle, (rest - middle.astype(F32)).astype(BF16)


def left3(x):
    high, low = split2(x)
    return jnp.concatenate([high, low, high], axis=1)


def right3(x, axis=0):
    high, low = split2(x)
    return jnp.concatenate([high, high, low], axis=axis)


def eliminate(r, at):
    groups = BLOCK // 8
    rows = lax.broadcasted_iota(jnp.int32, (8, 128), 0)
    base = (at // 128) * 128
    d = r[:, base : base + 128]
    cols = []
    for q in range(BLOCK):
        lane = at - base + q
        cols.append(
            {
                g: jnp.broadcast_to(d[8 * g : 8 * g + 8, lane : lane + 1], (8, 128))
                for g in range(q // 8, groups)
            }
        )
    width = r.shape[1] // 128
    rr = [
        [r[8 * g : 8 * g + 8, 128 * c : 128 * c + 128] for c in range(width)]
        for g in range(groups)
    ]

    def spread(v, s):
        return jnp.broadcast_to(v[s : s + 1, :], (8, 128))

    for p in range(BLOCK):
        gp, sp = p // 8, p % 8
        inverse = lax.rsqrt(spread(cols[p][gp], sp))
        column = {g: cols[p][g] * inverse for g in range(gp, groups)}
        for q in range(p + 1, BLOCK):
            b = spread(column[q // 8], q % 8)
            for g in range(q // 8, groups):
                cols[q][g] = cols[q][g] - column[g] * b
        below = dict(column)
        below[gp] = jnp.where(rows > sp, column[gp], 0.0)
        for c in range(width):
            row = spread(rr[gp][c], sp) * inverse
            for g in range(gp, groups):
                new = rr[g][c] - below[g] * row
                rr[g][c] = jnp.where(rows == sp, row, new) if g == gp else new
    return jnp.concatenate([jnp.concatenate(x, axis=1) for x in rr], axis=0)


def factor_stage(k, n, m_ref, u_ref, x_ref):
    o = k * BLOCK
    e = o + BLOCK
    r = eliminate(m_ref[o:e, :], o)
    at_row = lax.broadcasted_iota(jnp.int32, (BLOCK, n), 0) + o
    at_col = lax.broadcasted_iota(jnp.int32, (BLOCK, n), 1)
    u_ref[o:e, :] = jnp.where(at_col >= at_row, r[:, :n], 0.0)
    x_ref[o:e, :] = r[:, n:]
    if e < n:
        a0 = (e // 128) * 128
        h, m, l = split3(r)
        left = jnp.concatenate([h, h, m, h, l, m], axis=0)[:, a0:n]
        right = jnp.concatenate([h, m, h, l, h, m], axis=0)
        m_ref[e:n, :] = m_ref[e:n, :] - dot(left, right, TN)[e - a0 :, :]


def exchange_kernel(
    scale, batches, pan, tin, pt, tv, u, x, *rest,
):
    nb = len(batches)
    wf, rest = rest[:nb], rest[nb:]
    (ph, gb, gr, m, t_sem, own_sem, ps, pr, gs, grs, ws, wr), rest = rest[:12], rest[12:]
    wl, r1, r2, r3, r4 = (rest[nb * i : nb * i + nb] for i in range(5))
    n = pt.shape[0]
    rows = pt.shape[1]
    width = pan.shape[0]
    half = width // 2
    row, col = lax.axis_index("row"), lax.axis_index("col")
    y, xx = row // 4, row % 4
    z, core = col // 2, col % 2
    up, down = lax.rem(z + 1, 4), lax.rem(z + 3, 4)
    peer_up = (row, 2 * up + core)
    peer_down = (row, 2 * down + core)
    peer_core = (row, 2 * z + 1 - core)
    peers = (
        (4 * y + xx + 1 - 2 * (xx % 2), col),
        (4 * y + 3 - xx, col),
        (4 * (y + 1 - 2 * (y % 2)) + xx, col),
        (4 * (3 - y) + xx, col),
    )
    bits = ((xx + 1) // 2 % 2, xx // 2, (y + 1) // 2 % 2, y // 2)
    orders = ((0, 1, 2, 3), (1, 0, 3, 2), (2, 3, 0, 1), (3, 2, 1, 0))
    mesh = pl.DeviceIdType.MESH

    quarter = rows // 4
    loads = [
        pltpu.make_async_copy(tin.at[pl.ds(i * quarter, quarter)], tv.at[pl.ds(i * quarter, quarter)], t_sem.at[i])
        for i in range(4)
    ]
    own = pltpu.make_async_copy(pan, pt.at[pl.ds(width * col, width)], own_sem)
    own.start()
    barrier = pltpu.get_barrier_semaphore()
    for peer in (peer_up, peer_down, peer_core, *peers):
        pl.semaphore_signal(barrier, inc=1, device_id=peer, device_id_type=mesh)
    pl.semaphore_wait(barrier, 7)

    sent = []

    def send(src, dst, ssem, rsem, peer):
        copy = pltpu.make_async_remote_copy(src, dst, ssem, rsem, device_id=peer, device_id_type=mesh)
        copy.start()
        sent.append(copy)
        return copy

    def piece(c, part):
        return pt.at[pl.ds(width * c + half * part, half)]

    def forward(index, c, part, peer):
        return send(piece(c, part), piece(c, part), ps.at[index], pr.at[index], peer)

    p0 = send(pan.at[pl.ds(0, half)], piece(col, 0), ps.at[0], pr.at[0], peer_up)
    m0 = send(pan.at[pl.ds(half, half)], piece(col, 1), ps.at[1], pr.at[1], peer_down)
    p1 = send(pan.at[pl.ds(half, half)], piece(col, 1), ps.at[2], pr.at[2], peer_up)
    m1 = send(pan.at[pl.ds(0, half)], piece(col, 0), ps.at[3], pr.at[3], peer_down)
    c0 = send(pan, pt.at[pl.ds(width * col, width)], ps.at[4], pr.at[4], peer_core)
    for load in loads:
        load.start()
    c_down, c_up, c_far = 2 * down + core, 2 * up + core, 2 * lax.rem(z + 2, 4) + core
    p0.wait_recv()
    p2 = forward(5, c_down, 0, peer_up)
    f1 = forward(6, c_down, 0, peer_core)
    m0.wait_recv()
    m2 = forward(7, c_up, 1, peer_down)
    f2 = forward(8, c_up, 1, peer_core)
    p1.wait_recv()
    f3 = forward(9, c_down, 1, peer_core)
    m1.wait_recv()
    f4 = forward(10, c_up, 0, peer_core)
    p2.wait_recv()
    f5 = forward(11, c_far, 0, peer_core)
    m2.wait_recv()
    f6 = forward(12, c_far, 1, peer_core)
    own.wait()
    for copy in (c0, f1, f2, f3, f4, f5, f6):
        copy.wait_recv()

    whole = pt[...]
    ph[...] = left3(whole)
    gb[0] = dot(ph[...], right3(whole, 1), NT) * scale

    def gram_send(step):
        return [
            send(
                gb.at[step, pl.ds(64 * s, 64)], gr.at[step, pl.ds(64 * s, 64)],
                gs.at[step, s], grs.at[step, s], peers[orders[s][step]],
            )
            for s in range(4)
        ]

    def gram_add(step, copies):
        for s in range(4):
            at = slice(64 * s, 64 * s + 64)
            copies[s].wait_recv()
            if step < 3:
                gb[step + 1, at] = gb[step, at] + gr[step, at]
            else:
                m[at, :n] = gb[step, at] + gr[step, at]

    def product(b, i):
        j = batches[b][0] + i
        right = right3(tv[:, TILE * j : TILE * j + TILE])
        wl[b][:, TILE * i : TILE * i + TILE] = dot(ph[...], right, NN)

    kept, other = [], []
    for s in range(4):
        at = 64 * s
        k_s, o_s = [], []
        for level in range(3):
            size = 32 >> level
            b = bits[orders[s][level]]
            k_s.append(pl.multiple_of(at + size * b, 8))
            o_s.append(pl.multiple_of(at + size * (1 - b), 8))
            at = at + size * b
        kept.append(k_s)
        other.append(o_s)
    landing = (r1, r2, r3)
    flights = {}

    def product_send(b, level):
        copies = []
        for s in range(4):
            if level < 3:
                size = 32 >> level
                src = wl[b].at[pl.ds(other[s][level], size)]
                dst = landing[level][b].at[pl.ds(size * s, size)]
                axis = level
            elif level == 3:
                src = wl[b].at[pl.ds(kept[s][2], 8)]
                dst = r4[b].at[pl.ds(8 * s, 8)]
                axis = 3
            else:
                axis = 6 - level
                src = dst = wf[b].at[pl.ds(kept[s][axis], 32 >> axis)]
            copies.append(send(src, dst, ws.at[b, level, s], wr.at[b, level, s], peers[orders[s][axis]]))
        flights[b, level] = copies

    def product_step(b, level):
        for s in range(4):
            flights[b, level][s].wait_recv()
            if level < 3:
                size = 32 >> level
                at = pl.ds(kept[s][level], size)
                wl[b][at] = wl[b][at] + landing[level][b][size * s : size * s + size]
            elif level == 3:
                at = pl.ds(kept[s][2], 8)
                wf[b][at] = wl[b][at] + r4[b][8 * s : 8 * s + 8]
        if level < 6:
            product_send(b, level + 1)

    copies = gram_send(0)
    for load in loads:
        load.wait()
    product(0, 0)
    product(0, 1)
    gram_add(0, copies)
    copies = gram_send(1)
    product_send(0, 0)
    product(1, 0)
    product(1, 1)
    gram_add(1, copies)
    copies = gram_send(2)
    product(1, 2)
    product_send(1, 0)
    product_step(0, 0)
    gram_add(2, copies)
    copies = gram_send(3)
    product_step(1, 0)
    gram_add(3, copies)

    ri = lax.broadcasted_iota(jnp.int32, (n, n), 0)
    ci = lax.broadcasted_iota(jnp.int32, (n, n), 1)
    m[:, n:] = jnp.where(ri == ci, 1.0, 0.0).astype(F32)
    events = [(b, level) for level in range(1, 7) for b in (0, 1)]
    stages = n // BLOCK
    done = 0
    for k in range(stages):
        factor_stage(k, n, m, u, x)
        goal = (len(events) * (k + 1)) // stages
        while done < goal:
            product_step(*events[done])
            done += 1
    for copy in sent:
        copy.wait_send()


def exchange(panel_t, trailing, scale):
    width, rows = panel_t.shape
    n = width * 8
    tc = trailing.shape[1]
    batches = ((0, 2), (2, 5))
    widths = [TILE * (hi - lo) for lo, hi in batches]
    vm = pltpu.VMEM
    dma = pltpu.SemaphoreType.DMA
    return pl.pallas_call(
        functools.partial(exchange_kernel, scale, batches),
        out_shape=(vm((n, rows), F32), vm((rows, tc), F32), vm((n, n), F32), vm((n, n), F32), *(vm((n, c), F32) for c in widths)),
        in_specs=[pl.BlockSpec(memory_space=pltpu.HBM)] * 2,
        out_specs=(pl.BlockSpec(memory_space=pltpu.VMEM),) * (4 + len(batches)),
        scratch_shapes=[
            vm((n, 3 * rows), BF16),
            vm((4, n, n), F32),
            vm((4, n, n), F32),
            vm((n, 2 * n), F32),
            dma((4,)),
            dma,
            dma((13,)),
            dma((13,)),
            dma((4, 4)),
            dma((4, 4)),
            dma((2, 7, 4)),
            dma((2, 7, 4)),
            *(vm((size, c), F32) for size in (n, 128, 64, 32, 32) for c in widths),
        ],
        compiler_params=pltpu.CompilerParams(
            collective_id=0, has_side_effects=True, vmem_limit_bytes=36 * 2**20
        ),
        name="exchange",
    )(panel_t, trailing)


def update_kernel(inv_root, block, starts, pt, tv, u, x, *rest):
    ws, (u_out, q_out, r_out, t_out, r3, x3) = rest[:-6], rest[-6:]
    i = pl.program_id(0)

    @pl.when(i == 0)
    def _():
        left = left3(x[...])
        x3[...] = right3(x[...].T)
        for w, start in zip(ws, starts):
            for c in range(0, w.shape[1], TILE):
                r = dot(left, right3(w[:, c : c + TILE]), NN) * inv_root
                r_out[:, start + c : start + c + TILE] = r
                r3[:, start + c : start + c + TILE] = right3(r * inv_root)
        u_out[...] = u[...]

    at = pl.ds(pl.multiple_of(i * block, block), block)
    q = dot(left3(pt[:, at].T), x3[...], NN)
    q_out[...] = q
    q3 = left3(q)
    for c in range(0, r_out.shape[1], TILE):
        t_out[:, c : c + TILE] = tv[at, c : c + TILE] - dot(q3, r3[:, c : c + TILE], NN)


def update(pt, tv, u, x, ws, inv_root, block=256):
    n, rows = pt.shape
    tc = tv.shape[1]
    starts = [sum(w.shape[1] for w in ws[:i]) for i in range(len(ws))]
    resident = pl.BlockSpec(memory_space=pltpu.VMEM)

    def whole(*shape):
        return pl.BlockSpec(shape, lambda i: (0, 0))

    def by_rows(width):
        return pl.BlockSpec((block, width), lambda i: (i, 0))

    return pl.pallas_call(
        functools.partial(update_kernel, inv_root, block, starts),
        grid=(rows // block,),
        out_shape=(
            jax.ShapeDtypeStruct((n, n), F32),
            jax.ShapeDtypeStruct((rows, n), F32),
            jax.ShapeDtypeStruct((n, tc), F32),
            jax.ShapeDtypeStruct((rows, tc), F32),
        ),
        in_specs=[resident] * (4 + len(ws)),
        out_specs=(whole(n, n), by_rows(n), whole(n, tc), by_rows(tc)),
        scratch_shapes=[pltpu.VMEM((3 * n, tc), BF16), pltpu.VMEM((3 * n, n), BF16)],
        compiler_params=pltpu.CompilerParams(vmem_limit_bytes=20 * 2**20),
        name="update",
    )(pt, tv, u, x, *ws)


def per_device(panel, trailing_in):
    rows_all = panel.shape[0] * lax.axis_size("row")
    pt, tv, u, x, *ws = exchange(panel.T, trailing_in, 1.0 / rows_all)
    return update(pt, tv, u, x, ws, 1.0 / math.sqrt(rows_all))


def solution(mesh):
    in_specs = (P("row", "col"), P("row", "col"))
    out_specs = (P(), P("row", None), P(None, "col"), P("row", "col"))
    return jax.shard_map(
        per_device, mesh=mesh, in_specs=in_specs, out_specs=out_specs, check_vma=False
    )
```

```python
import functools
import math

import jax
import jax.numpy as jnp
from jax import lax
from jax.experimental import pallas as pl
from jax.experimental.pallas import tpu as pltpu
from jax.sharding import PartitionSpec as P

F32 = jnp.float32
BF16 = jnp.bfloat16
NN = (((1,), (0,)), ((), ()))
NT = (((1,), (1,)), ((), ()))
TN = (((0,), (0,)), ((), ()))
BLOCK = 32
TILE = 256
dot = functools.partial(lax.dot_general, preferred_element_type=F32)


def split2(x):
    high = x.astype(BF16)
    return high, (x - high.astype(F32)).astype(BF16)


def split3(x):
    high = x.astype(BF16)
    rest = x - high.astype(F32)
    middle = rest.astype(BF16)
    return high, middle, (rest - middle.astype(F32)).astype(BF16)


def left3(x):
    high, low = split2(x)
    return jnp.concatenate([high, low, high], axis=1)


def right3(x, axis=0):
    high, low = split2(x)
    return jnp.concatenate([high, high, low], axis=axis)


def eliminate(r, at):
    groups = BLOCK // 8
    rows = lax.broadcasted_iota(jnp.int32, (8, 128), 0)
    base = (at // 128) * 128
    d = r[:, base : base + 128]
    cols = []
    for q in range(BLOCK):
        lane = at - base + q
        cols.append(
            {
                g: jnp.broadcast_to(d[8 * g : 8 * g + 8, lane : lane + 1], (8, 128))
                for g in range(q // 8, groups)
            }
        )
    width = r.shape[1] // 128
    rr = [
        [r[8 * g : 8 * g + 8, 128 * c : 128 * c + 128] for c in range(width)]
        for g in range(groups)
    ]

    def spread(v, s):
        return jnp.broadcast_to(v[s : s + 1, :], (8, 128))

    for p in range(BLOCK):
        gp, sp = p // 8, p % 8
        inverse = lax.rsqrt(spread(cols[p][gp], sp))
        column = {g: cols[p][g] * inverse for g in range(gp, groups)}
        for q in range(p + 1, BLOCK):
            b = spread(column[q // 8], q % 8)
            for g in range(q // 8, groups):
                cols[q][g] = cols[q][g] - column[g] * b
        below = dict(column)
        below[gp] = jnp.where(rows > sp, column[gp], 0.0)
        for c in range(width):
            row = spread(rr[gp][c], sp) * inverse
            for g in range(gp, groups):
                new = rr[g][c] - below[g] * row
                rr[g][c] = jnp.where(rows == sp, row, new) if g == gp else new
    return jnp.concatenate([jnp.concatenate(x, axis=1) for x in rr], axis=0)


def factor_stage(k, n, m_ref, u_ref, x_ref):
    o = k * BLOCK
    e = o + BLOCK
    r = eliminate(m_ref[o:e, :], o)
    at_row = lax.broadcasted_iota(jnp.int32, (BLOCK, n), 0) + o
    at_col = lax.broadcasted_iota(jnp.int32, (BLOCK, n), 1)
    u_ref[o:e, :] = jnp.where(at_col >= at_row, r[:, :n], 0.0)
    x_ref[o:e, :] = r[:, n:]
    if e < n:
        a0 = (e // 128) * 128
        h, m, l = split3(r)
        left = jnp.concatenate([h, h, m, h, l, m], axis=0)[:, a0:n]
        right = jnp.concatenate([h, m, h, l, h, m], axis=0)
        m_ref[e:n, :] = m_ref[e:n, :] - dot(left, right, TN)[e - a0 :, :]


def exchange_kernel(
    scale, pan, tin, pt, tv, u, x, wf, th, tl, ph, gb, gr, gf, m, wl, w4, r1, r2, r3, r4,
    t_sem, own_sem, ps, pr, gs, grs, es, er, ws, wr,
):
    n, rows = pt.shape
    width = pan.shape[0]
    half = width // 2
    tc = tv.shape[1]
    part = tc // 2
    row, col = lax.axis_index("row"), lax.axis_index("col")
    y, xx = row // 4, row % 4
    z, core = col // 2, col % 2
    up, down, far = lax.rem(z + 1, 4), lax.rem(z + 3, 4), lax.rem(z + 2, 4)
    peer_up = (row, 2 * up + core)
    peer_down = (row, 2 * down + core)
    peer_core = (row, 2 * z + 1 - core)
    peers = (
        (4 * y + xx + 1 - 2 * (xx % 2), col),
        (4 * y + 3 - xx, col),
        (4 * (y + 1 - 2 * (y % 2)) + xx, col),
        (4 * (3 - y) + xx, col),
    )
    bits = ((xx + 1) // 2 % 2, xx // 2, (y + 1) // 2 % 2, y // 2)
    orders = ((0, 1, 2, 3), (1, 0, 3, 2), (2, 3, 0, 1), (3, 2, 1, 0))
    mesh = pl.DeviceIdType.MESH

    quarter = rows // 4
    loads = [
        pltpu.make_async_copy(tin.at[pl.ds(i * quarter, quarter)], tv.at[pl.ds(i * quarter, quarter)], t_sem.at[i])
        for i in range(4)
    ]
    own = pltpu.make_async_copy(pan, pt.at[pl.ds(width * col, width)], own_sem)
    own.start()
    barrier = pltpu.get_barrier_semaphore()
    for peer in (peer_up, peer_down, peer_core, *peers):
        pl.semaphore_signal(barrier, inc=1, device_id=peer, device_id_type=mesh)
    pl.semaphore_wait(barrier, 7)

    sent = []

    def send(src, dst, ssem, rsem, peer):
        copy = pltpu.make_async_remote_copy(src, dst, ssem, rsem, device_id=peer, device_id_type=mesh)
        copy.start()
        sent.append(copy)
        return copy

    def piece(c, side):
        return pt.at[pl.ds(width * c + half * side, half)]

    def forward(index, c, side, peer):
        return send(piece(c, side), piece(c, side), ps.at[index], pr.at[index], peer)

    p0 = send(pan.at[pl.ds(0, half)], piece(col, 0), ps.at[0], pr.at[0], peer_up)
    m0 = send(pan.at[pl.ds(half, half)], piece(col, 1), ps.at[1], pr.at[1], peer_down)
    p1 = send(pan.at[pl.ds(half, half)], piece(col, 1), ps.at[2], pr.at[2], peer_up)
    m1 = send(pan.at[pl.ds(0, half)], piece(col, 0), ps.at[3], pr.at[3], peer_down)
    c0 = send(pan, pt.at[pl.ds(width * col, width)], ps.at[4], pr.at[4], peer_core)
    for load in loads:
        load.start()
    c_down, c_up, c_far = 2 * down + core, 2 * up + core, 2 * far + core

    starts = [pl.multiple_of(2 * width * q, 64) for q in (z, down, up, far)]
    tall = 2 * width

    def split_panel(b):
        at = pl.ds(starts[b], tall)
        ph[0, at], ph[1, at] = split2(pt[at])

    def product(bs, j):
        cols = slice(TILE * j, TILE * j + TILE)
        high = [ph[0, pl.ds(starts[b], tall)] for b in bs]
        low = [ph[1, pl.ds(starts[b], tall)] for b in bs]
        size = tall * len(bs)
        both = dot(jnp.concatenate(high + low, axis=0), th[:, cols], NN)
        total = both[:size] + (both[size:] + dot(jnp.concatenate(high, axis=0), tl[:, cols], NN))
        for i, b in enumerate(bs):
            wl[b, :, cols] = total[tall * i : tall * i + tall]

    keep_row = [pl.multiple_of(16 * s + 8 * bits[orders[s][0]], 8) for s in range(4)]
    give_row = [pl.multiple_of(16 * s + 8 - 8 * bits[orders[s][0]], 8) for s in range(4)]
    keep_col = [pl.multiple_of(part * bits[orders[s][1]], 128) for s in range(4)]
    give_col = [pl.multiple_of(part - part * bits[orders[s][1]], 128) for s in range(4)]
    axes = (0, 1, 2, 3, 1, 0)
    flights = {}

    def product_send(b, level):
        copies = []
        for s in range(4):
            slot = pl.ds(8 * s, 8)
            kept, lanes = pl.ds(keep_row[s], 8), pl.ds(keep_col[s], part)
            final = pl.ds(pl.multiple_of(starts[b] + keep_row[s], 8), 8)
            if level == 0:
                src, dst = wl.at[b, pl.ds(give_row[s], 8)], r1.at[b, slot]
            elif level == 1:
                src, dst = wl.at[b, kept, pl.ds(give_col[s], part)], r2.at[b, slot]
            elif level == 2:
                src, dst = wl.at[b, kept, lanes], r3.at[b, slot]
            elif level == 3:
                src, dst = w4.at[b, slot], r4.at[b, slot]
            elif level == 4:
                src = dst = wf.at[final, lanes]
            else:
                src = dst = wf.at[final]
            copies.append(send(src, dst, ws.at[b, level, s], wr.at[b, level, s], peers[orders[s][axes[level]]]))
        flights[b, level] = copies

    def product_step(b, level):
        for s in range(4):
            flights[b, level][s].wait_recv()
            slot = slice(8 * s, 8 * s + 8)
            kept, lanes = pl.ds(keep_row[s], 8), pl.ds(keep_col[s], part)
            final = pl.ds(pl.multiple_of(starts[b] + keep_row[s], 8), 8)
            if level == 0:
                wl[b, kept] = wl[b, kept] + r1[b, slot]
            elif level == 1:
                wl[b, kept, lanes] = wl[b, kept, lanes] + r2[b, slot]
            elif level == 2:
                w4[b, slot] = wl[b, kept, lanes] + r3[b, slot]
            elif level == 3:
                wf[final, lanes] = w4[b, slot] + r4[b, slot]
        if level < 5:
            product_send(b, level + 1)

    deep = n // 2
    piled = deep // 4
    half_at = pl.multiple_of(deep * core, deep)

    def gram_local():
        high, low = ph[0, pl.ds(half_at, deep)], ph[1, pl.ds(half_at, deep)]
        both = dot(jnp.concatenate([high, low], axis=0), ph[0], NT)
        gb[0] = (both[:deep] + (both[deep:] + dot(high, ph[1], NT))) * scale

    def gram_send(step):
        return [
            send(
                gb.at[step, pl.ds(piled * s, piled)], gr.at[step, pl.ds(piled * s, piled)],
                gs.at[step, s], grs.at[step, s], peers[orders[s][step]],
            )
            for s in range(4)
        ]

    def gram_add(step, copies):
        for s in range(4):
            at = slice(piled * s, piled * s + piled)
            copies[s].wait_recv()
            total = gb[step, at] + gr[step, at]
            if step < 3:
                gb[step + 1, at] = total
            else:
                gf[pl.ds(pl.multiple_of(half_at + piled * s, piled), piled)] = total

    own.wait()
    c0.wait_recv()
    split_panel(0)
    p0.wait_recv()
    p2 = forward(5, c_down, 0, peer_up)
    f1 = forward(6, c_down, 0, peer_core)
    m0.wait_recv()
    m2 = forward(7, c_up, 1, peer_down)
    f2 = forward(8, c_up, 1, peer_core)
    for i in range(4):
        loads[i].wait()

        @pl.loop(0, quarter // 64)
        def _(k, i=i):
            at = pl.ds(pl.multiple_of(i * quarter + k * 64, 64), 64)
            th[at], tl[at] = split2(tv[at])

    for j in range(tc // TILE):
        product((0,), j)
    product_send(0, 0)
    p1.wait_recv()
    f3 = forward(9, c_down, 1, peer_core)
    m1.wait_recv()
    f4 = forward(10, c_up, 0, peer_core)
    for copy in (f1, f2, f3, f4):
        copy.wait_recv()
    split_panel(1)
    split_panel(2)
    p2.wait_recv()
    f5 = forward(11, c_far, 0, peer_core)
    m2.wait_recv()
    f6 = forward(12, c_far, 1, peer_core)
    f5.wait_recv()
    f6.wait_recv()
    split_panel(3)
    gram_local()
    copies = gram_send(0)
    product_step(0, 0)
    for j in range(4):
        product((1, 2), j)
    gram_add(0, copies)
    copies = gram_send(1)
    product_step(0, 1)
    product((1, 2), 4)
    product_send(1, 0)
    product_send(2, 0)
    product((3,), 0)
    product((3,), 1)
    product((3,), 2)
    gram_add(1, copies)
    copies = gram_send(2)
    product((3,), 3)
    product((3,), 4)
    product_send(3, 0)
    product_step(0, 2)
    product_step(1, 0)
    gram_add(2, copies)
    copies = gram_send(3)
    product_step(2, 0)
    product_step(0, 3)
    gram_add(3, copies)
    mine = gf.at[pl.ds(half_at, deep)]
    swap = send(mine, mine, es, er, peer_core)
    product_step(3, 0)
    ri = lax.broadcasted_iota(jnp.int32, (n, n), 0)
    ci = lax.broadcasted_iota(jnp.int32, (n, n), 1)
    m[:, n:] = jnp.where(ri == ci, 1.0, 0.0).astype(F32)
    swap.wait_recv()
    m[:, :n] = gf[...]

    events = [
        (1, 1), (2, 1), (0, 4), (3, 1), (1, 2), (2, 2), (0, 5), (3, 2), (1, 3), (2, 3), (3, 3), (1, 4), (2, 4), (3, 4),
        (1, 5), (2, 5), (3, 5),
    ]
    stages = n // BLOCK
    done = 0
    for k in range(stages):
        factor_stage(k, n, m, u, x)
        goal = (len(events) * (k + 1)) // stages
        while done < goal:
            product_step(*events[done])
            done += 1
    for copy in sent:
        copy.wait_send()


def exchange(panel_t, trailing, scale):
    width, rows = panel_t.shape
    n = width * 8
    tc = trailing.shape[1]
    vm = pltpu.VMEM
    dma = pltpu.SemaphoreType.DMA
    return pl.pallas_call(
        functools.partial(exchange_kernel, scale),
        out_shape=(vm((n, rows), F32), vm((rows, tc), F32), vm((n, n), F32), vm((n, n), F32), vm((n, tc), F32)),
        in_specs=[pl.BlockSpec(memory_space=pltpu.HBM)] * 2,
        out_specs=(pl.BlockSpec(memory_space=pltpu.VMEM),) * 5,
        scratch_shapes=[
            vm((rows, tc), BF16),
            vm((rows, tc), BF16),
            vm((2, n, rows), BF16),
            vm((4, n // 2, n), F32),
            vm((4, n // 2, n), F32),
            vm((n, n), F32),
            vm((n, 2 * n), F32),
            vm((4, 2 * width, tc), F32),
            vm((4, 32, tc // 2), F32),
            vm((4, 32, tc), F32),
            vm((4, 32, tc // 2), F32),
            vm((4, 32, tc // 2), F32),
            vm((4, 32, tc // 2), F32),
            dma((4,)),
            dma,
            dma((13,)),
            dma((13,)),
            dma((4, 4)),
            dma((4, 4)),
            dma,
            dma,
            dma((4, 6, 4)),
            dma((4, 6, 4)),
        ],
        compiler_params=pltpu.CompilerParams(
            collective_id=0, has_side_effects=True, vmem_limit_bytes=36 * 2**20
        ),
        name="exchange",
    )(panel_t, trailing)


def update_kernel(inv_root, block, pt, tv, u, x, w, u_out, q_out, r_out, t_out, r3, x3):
    i = pl.program_id(0)

    @pl.when(i == 0)
    def _():
        left = left3(x[...])
        x3[...] = right3(x[...].T)
        for c in range(0, w.shape[1], TILE):
            r = dot(left, right3(w[:, c : c + TILE]), NN) * inv_root
            r_out[:, c : c + TILE] = r
            r3[:, c : c + TILE] = right3(r * inv_root)
        u_out[...] = u[...]

    at = pl.ds(pl.multiple_of(i * block, block), block)
    q = dot(left3(pt[:, at].T), x3[...], NN)
    q_out[...] = q
    q3 = left3(q)
    for c in range(0, r_out.shape[1], TILE):
        t_out[:, c : c + TILE] = tv[at, c : c + TILE] - dot(q3, r3[:, c : c + TILE], NN)


def update(pt, tv, u, x, w, inv_root, block=256):
    n, rows = pt.shape
    tc = tv.shape[1]
    resident = pl.BlockSpec(memory_space=pltpu.VMEM)

    def whole(*shape):
        return pl.BlockSpec(shape, lambda i: (0, 0))

    def by_rows(width):
        return pl.BlockSpec((block, width), lambda i: (i, 0))

    return pl.pallas_call(
        functools.partial(update_kernel, inv_root, block),
        grid=(rows // block,),
        out_shape=(
            jax.ShapeDtypeStruct((n, n), F32),
            jax.ShapeDtypeStruct((rows, n), F32),
            jax.ShapeDtypeStruct((n, tc), F32),
            jax.ShapeDtypeStruct((rows, tc), F32),
        ),
        in_specs=[resident] * 5,
        out_specs=(whole(n, n), by_rows(n), whole(n, tc), by_rows(tc)),
        scratch_shapes=[pltpu.VMEM((3 * n, tc), BF16), pltpu.VMEM((3 * n, n), BF16)],
        compiler_params=pltpu.CompilerParams(vmem_limit_bytes=20 * 2**20),
        name="update",
    )(pt, tv, u, x, w)


def per_device(panel, trailing_in):
    rows_all = panel.shape[0] * lax.axis_size("row")
    pt, tv, u, x, w = exchange(panel.T, trailing_in, 1.0 / rows_all)
    return update(pt, tv, u, x, w, 1.0 / math.sqrt(rows_all))


def solution(mesh):
    in_specs = (P("row", "col"), P("row", "col"))
    out_specs = (P(), P("row", None), P(None, "col"), P("row", "col"))
    return jax.shard_map(
        per_device, mesh=mesh, in_specs=in_specs, out_specs=out_specs, check_vma=False
    )
```

```python
import functools
import math

import jax
import jax.numpy as jnp
from jax import lax
from jax.experimental import pallas as pl
from jax.experimental.pallas import tpu as pltpu
from jax.sharding import PartitionSpec as P

F32 = jnp.float32
BF16 = jnp.bfloat16
NN = (((1,), (0,)), ((), ()))
NT = (((1,), (1,)), ((), ()))
TN = (((0,), (0,)), ((), ()))
BLOCK = 32
TILE = 256
dot = functools.partial(lax.dot_general, preferred_element_type=F32)


def split2(x):
    high = x.astype(BF16)
    return high, (x - high.astype(F32)).astype(BF16)


def split3(x):
    high = x.astype(BF16)
    rest = x - high.astype(F32)
    middle = rest.astype(BF16)
    return high, middle, (rest - middle.astype(F32)).astype(BF16)


def left3(x):
    high, low = split2(x)
    return jnp.concatenate([high, low, high], axis=1)


def right3(x, axis=0):
    high, low = split2(x)
    return jnp.concatenate([high, high, low], axis=axis)


def eliminate(r, at):
    groups = BLOCK // 8
    rows = lax.broadcasted_iota(jnp.int32, (8, 128), 0)
    base = (at // 128) * 128
    d = r[:, base : base + 128]
    cols = []
    for q in range(BLOCK):
        lane = at - base + q
        cols.append(
            {
                g: jnp.broadcast_to(d[8 * g : 8 * g + 8, lane : lane + 1], (8, 128))
                for g in range(q // 8, groups)
            }
        )
    width = r.shape[1] // 128
    rr = [
        [r[8 * g : 8 * g + 8, 128 * c : 128 * c + 128] for c in range(width)]
        for g in range(groups)
    ]

    def spread(v, s):
        return jnp.broadcast_to(v[s : s + 1, :], (8, 128))

    for p in range(BLOCK):
        gp, sp = p // 8, p % 8
        inverse = lax.rsqrt(spread(cols[p][gp], sp))
        column = {g: cols[p][g] * inverse for g in range(gp, groups)}
        for q in range(p + 1, BLOCK):
            b = spread(column[q // 8], q % 8)
            for g in range(q // 8, groups):
                cols[q][g] = cols[q][g] - column[g] * b
        below = dict(column)
        below[gp] = jnp.where(rows > sp, column[gp], 0.0)
        for c in range(width):
            row = spread(rr[gp][c], sp) * inverse
            for g in range(gp, groups):
                new = rr[g][c] - below[g] * row
                rr[g][c] = jnp.where(rows == sp, row, new) if g == gp else new
    return jnp.concatenate([jnp.concatenate(x, axis=1) for x in rr], axis=0)


def factor_stage(k, n, m_ref, u_ref, x_ref):
    o = k * BLOCK
    e = o + BLOCK
    r = eliminate(m_ref[o:e, :], o)
    at_row = lax.broadcasted_iota(jnp.int32, (BLOCK, n), 0) + o
    at_col = lax.broadcasted_iota(jnp.int32, (BLOCK, n), 1)
    u_ref[o:e, :] = jnp.where(at_col >= at_row, r[:, :n], 0.0)
    x_ref[o:e, :] = r[:, n:]
    if e < n:
        a0 = (e // 128) * 128
        h, m, l = split3(r)
        left = jnp.concatenate([h, h, m, h, l, m], axis=0)[:, a0:n]
        right = jnp.concatenate([h, m, h, l, h, m], axis=0)
        m_ref[e:n, :] = m_ref[e:n, :] - dot(left, right, TN)[e - a0 :, :]


def exchange_kernel(
    scale, pan, tin, pt, tv, u, x, wf, th, tl, ph, g1, g2, gf, m, wl, r1, r2,
    t_sem, own_sem, ps, pr, gs, grs, es, er, ws, wr,
):
    n, rows = pt.shape
    width = pan.shape[0]
    half = width // 2
    tc = tv.shape[1]
    row, col = lax.axis_index("row"), lax.axis_index("col")
    y, xx = row // 4, row % 4
    z, core = col // 2, col % 2
    up, down, far = lax.rem(z + 1, 4), lax.rem(z + 3, 4), lax.rem(z + 2, 4)
    peer_up = (row, 2 * up + core)
    peer_down = (row, 2 * down + core)
    peer_core = (row, 2 * z + 1 - core)
    place = (xx, y)

    def on_ring(axis, ahead):
        if axis == 0:
            return (4 * y + lax.rem(xx + ahead, 4), col)
        return (4 * lax.rem(y + ahead, 4) + xx, col)

    mesh = pl.DeviceIdType.MESH

    quarter = rows // 4
    loads = [
        pltpu.make_async_copy(tin.at[pl.ds(i * quarter, quarter)], tv.at[pl.ds(i * quarter, quarter)], t_sem.at[i])
        for i in range(4)
    ]
    own = pltpu.make_async_copy(pan, pt.at[pl.ds(width * col, width)], own_sem)
    own.start()
    barrier = pltpu.get_barrier_semaphore()
    around = [on_ring(axis, ahead) for axis in (0, 1) for ahead in (1, 2, 3)]
    for peer in (peer_up, peer_down, peer_core, *around):
        pl.semaphore_signal(barrier, inc=1, device_id=peer, device_id_type=mesh)
    pl.semaphore_wait(barrier, 9)

    sent = []

    def send(src, dst, ssem, rsem, peer):
        copy = pltpu.make_async_remote_copy(src, dst, ssem, rsem, device_id=peer, device_id_type=mesh)
        copy.start()
        sent.append(copy)
        return copy

    def piece(c, side):
        return pt.at[pl.ds(width * c + half * side, half)]

    def forward(index, c, side, peer):
        return send(piece(c, side), piece(c, side), ps.at[index], pr.at[index], peer)

    p0 = send(pan.at[pl.ds(0, half)], piece(col, 0), ps.at[0], pr.at[0], peer_up)
    m0 = send(pan.at[pl.ds(half, half)], piece(col, 1), ps.at[1], pr.at[1], peer_down)
    p1 = send(pan.at[pl.ds(half, half)], piece(col, 1), ps.at[2], pr.at[2], peer_up)
    m1 = send(pan.at[pl.ds(0, half)], piece(col, 0), ps.at[3], pr.at[3], peer_down)
    c0 = send(pan, pt.at[pl.ds(width * col, width)], ps.at[4], pr.at[4], peer_core)
    for load in loads:
        load.start()
    c_down, c_up, c_far = 2 * down + core, 2 * up + core, 2 * far + core

    starts = [pl.multiple_of(2 * width * q, 64) for q in (z, down, up, far)]
    tall = 2 * width

    def split_panel(b):
        at = pl.ds(starts[b], tall)
        ph[0, at], ph[1, at] = split2(pt[at])

    def product(bs, j):
        cols = slice(TILE * j, TILE * j + TILE)
        high = [ph[0, pl.ds(starts[b], tall)] for b in bs]
        low = [ph[1, pl.ds(starts[b], tall)] for b in bs]
        size = tall * len(bs)
        both = dot(jnp.concatenate(high + low, axis=0), th[:, cols], NN)
        total = both[:size] + (both[size:] + dot(jnp.concatenate(high, axis=0), tl[:, cols], NN))
        for i, b in enumerate(bs):
            wl[b, :, cols] = total[tall * i : tall * i + tall]

    short = 8
    flights = {}

    def product_send(b, phase):
        copies = []
        for h in (0, 1):
            axis = (h + phase) % 2
            first = pl.multiple_of(starts[b] + 32 * h + short * place[h], short)
            for ahead in (2, 1, 3):
                there = lax.rem(place[axis] + ahead, 4)
                if phase == 0:
                    src = wl.at[b, pl.ds(pl.multiple_of(32 * h + short * there, short), short)]
                    dst = r1.at[b, h, ahead - 1]
                elif phase == 1:
                    src = dst = r2.at[b, h, place[axis]]
                else:
                    src = dst = wf.at[pl.ds(first, short)]
                ssem, rsem = ws.at[b, phase, h, ahead - 1], wr.at[b, phase, h, ahead - 1]
                copies.append(send(src, dst, ssem, rsem, on_ring(axis, ahead)))
        flights[b, phase] = copies

    def product_step(b, phase):
        for copy in flights[b, phase]:
            copy.wait_recv()
        for h in (0, 1):
            first = pl.multiple_of(starts[b] + 32 * h + short * place[h], short)
            if phase == 0:
                mine = wl[b, pl.ds(pl.multiple_of(32 * h + short * place[h], short), short)]
                r2[b, h, place[1 - h]] = (mine + r1[b, h, 0]) + (r1[b, h, 1] + r1[b, h, 2])
            elif phase == 1:
                wf[pl.ds(first, short)] = (r2[b, h, 0] + r2[b, h, 1]) + (r2[b, h, 2] + r2[b, h, 3])
        if phase < 2:
            product_send(b, phase + 1)

    deep = n // 2
    piled = deep // 2
    half_at = pl.multiple_of(deep * core, deep)
    gram = (g1, g2)

    def gram_local():
        high, low = ph[0, pl.ds(half_at, deep)], ph[1, pl.ds(half_at, deep)]
        both = dot(jnp.concatenate([high, low], axis=0), ph[0], NT)
        total = (both[:deep] + (both[deep:] + dot(high, ph[1], NT))) * scale
        for h in (0, 1):
            g1[h, place[h]] = total[piled * h : piled * h + piled]

    def gram_send(phase):
        copies = []
        for h in (0, 1):
            axis = (h + phase) % 2
            for ahead in (2, 1, 3):
                mine = gram[phase].at[h, place[axis]]
                ssem, rsem = gs.at[phase, h, ahead - 1], grs.at[phase, h, ahead - 1]
                copies.append(send(mine, mine, ssem, rsem, on_ring(axis, ahead)))
        return copies

    def gram_add(phase, copies):
        for copy in copies:
            copy.wait_recv()
        for h in (0, 1):
            g = gram[phase]
            total = (g[h, 0] + g[h, 1]) + (g[h, 2] + g[h, 3])
            if phase == 0:
                g2[h, place[1 - h]] = total
            else:
                gf[pl.ds(pl.multiple_of(half_at + piled * h, piled), piled)] = total

    own.wait()
    c0.wait_recv()
    split_panel(0)
    p0.wait_recv()
    p2 = forward(5, c_down, 0, peer_up)
    f1 = forward(6, c_down, 0, peer_core)
    m0.wait_recv()
    m2 = forward(7, c_up, 1, peer_down)
    f2 = forward(8, c_up, 1, peer_core)
    for i in range(4):
        loads[i].wait()

        @pl.loop(0, quarter // 64)
        def _(k, i=i):
            at = pl.ds(pl.multiple_of(i * quarter + k * 64, 64), 64)
            th[at], tl[at] = split2(tv[at])

    for j in range(tc // TILE):
        product((0,), j)
    product_send(0, 0)
    p1.wait_recv()
    f3 = forward(9, c_down, 1, peer_core)
    m1.wait_recv()
    f4 = forward(10, c_up, 0, peer_core)
    for copy in (f1, f2, f3, f4):
        copy.wait_recv()
    split_panel(1)
    split_panel(2)
    for j in range(3):
        product((1, 2), j)
    p2.wait_recv()
    f5 = forward(11, c_far, 0, peer_core)
    m2.wait_recv()
    f6 = forward(12, c_far, 1, peer_core)
    for j in range(3, tc // TILE):
        product((1, 2), j)
    f5.wait_recv()
    f6.wait_recv()
    split_panel(3)
    gram_local()
    copies = gram_send(0)
    product_send(1, 0)
    product_send(2, 0)
    product_step(0, 0)
    for j in range(tc // TILE):
        product((3,), j)
    gram_add(0, copies)
    copies = gram_send(1)
    product_send(3, 0)
    product_step(1, 0)
    product_step(2, 0)
    product_step(0, 1)
    gram_add(1, copies)
    mine = gf.at[pl.ds(half_at, deep)]
    swap = send(mine, mine, es, er, peer_core)
    ri = lax.broadcasted_iota(jnp.int32, (n, n), 0)
    ci = lax.broadcasted_iota(jnp.int32, (n, n), 1)
    m[:, n:] = jnp.where(ri == ci, 1.0, 0.0).astype(F32)
    product_step(3, 0)
    swap.wait_recv()
    m[:, :n] = gf[...]

    events = [(1, 1), (2, 1), (0, 2), (3, 1), (1, 2), (2, 2), (3, 2)]
    stages = n // BLOCK
    done = 0
    for k in range(stages):
        factor_stage(k, n, m, u, x)
        goal = (len(events) * (k + 1)) // stages
        while done < goal:
            product_step(*events[done])
            done += 1
    for copy in sent:
        copy.wait_send()


def exchange(panel_t, trailing, scale):
    width, rows = panel_t.shape
    n = width * 8
    tc = trailing.shape[1]
    vm = pltpu.VMEM
    dma = pltpu.SemaphoreType.DMA
    return pl.pallas_call(
        functools.partial(exchange_kernel, scale),
        out_shape=(vm((n, rows), F32), vm((rows, tc), F32), vm((n, n), F32), vm((n, n), F32), vm((n, tc), F32)),
        in_specs=[pl.BlockSpec(memory_space=pltpu.HBM)] * 2,
        out_specs=(pl.BlockSpec(memory_space=pltpu.VMEM),) * 5,
        scratch_shapes=[
            vm((rows, tc), BF16),
            vm((rows, tc), BF16),
            vm((2, n, rows), BF16),
            vm((2, 4, n // 4, n), F32),
            vm((2, 4, n // 4, n), F32),
            vm((n, n), F32),
            vm((n, 2 * n), F32),
            vm((4, 2 * width, tc), F32),
            vm((4, 2, 3, 8, tc), F32),
            vm((4, 2, 4, 8, tc), F32),
            dma((4,)),
            dma,
            dma((13,)),
            dma((13,)),
            dma((2, 2, 3)),
            dma((2, 2, 3)),
            dma,
            dma,
            dma((4, 3, 2, 3)),
            dma((4, 3, 2, 3)),
        ],
        compiler_params=pltpu.CompilerParams(
            collective_id=0, has_side_effects=True, vmem_limit_bytes=36 * 2**20
        ),
        name="exchange",
    )(panel_t, trailing)


def update_kernel(inv_root, pt, tv, u, x, w, u_out, q_out, r_out, t_out, q3, r3, x3):
    i, j = pl.program_id(0), pl.program_id(1)
    block, tile = t_out.shape
    rows = pl.ds(pl.multiple_of(i * block, block), block)
    cols = pl.ds(pl.multiple_of(j * tile, tile), tile)

    @pl.when((i == 0) & (j == 0))
    def _():
        x3[...] = right3(x[...].T)
        u_out[...] = u[...]

    @pl.when(i == 0)
    def _():
        r = dot(left3(x[...]), right3(w[:, cols]), NN) * inv_root
        r_out[...] = r
        r3[:, cols] = right3(r * inv_root)

    @pl.when(j == 0)
    def _():
        q = dot(left3(pt[:, rows].T), x3[...], NN)
        q_out[...] = q
        q3[...] = left3(q)

    t_out[...] = tv[rows, cols] - dot(q3[...], r3[:, cols], NN)


def update(pt, tv, u, x, w, inv_root, block=512):
    n, rows = pt.shape
    tc = tv.shape[1]
    tiles = tc // TILE
    resident = pl.BlockSpec(memory_space=pltpu.VMEM)
    return pl.pallas_call(
        functools.partial(update_kernel, inv_root),
        grid=(rows // block, tiles),
        out_shape=(
            jax.ShapeDtypeStruct((n, n), F32),
            jax.ShapeDtypeStruct((rows, n), F32),
            jax.ShapeDtypeStruct((n, tc), F32),
            jax.ShapeDtypeStruct((rows, tc), F32),
        ),
        in_specs=[resident] * 5,
        out_specs=(
            pl.BlockSpec((n, n), lambda i, j: (0, 0)),
            pl.BlockSpec((block, n), lambda i, j: (i, 0)),
            pl.BlockSpec((n, TILE), lambda i, j: (0, jnp.where(i == 0, j, tiles - 1))),
            pl.BlockSpec((block, TILE), lambda i, j: (i, j)),
        ),
        scratch_shapes=[
            pltpu.VMEM((block, 3 * n), BF16),
            pltpu.VMEM((3 * n, tc), BF16),
            pltpu.VMEM((3 * n, n), BF16),
        ],
        compiler_params=pltpu.CompilerParams(vmem_limit_bytes=20 * 2**20),
        name="update",
    )(pt, tv, u, x, w)


def per_device(panel, trailing_in):
    rows_all = panel.shape[0] * lax.axis_size("row")
    pt, tv, u, x, w = exchange(panel.T, trailing_in, 1.0 / rows_all)
    return update(pt, tv, u, x, w, 1.0 / math.sqrt(rows_all))


def solution(mesh):
    in_specs = (P("row", "col"), P("row", "col"))
    out_specs = (P(), P("row", None), P(None, "col"), P("row", "col"))
    return jax.shard_map(
        per_device, mesh=mesh, in_specs=in_specs, out_specs=out_specs, check_vma=False
    )
```

```python
import functools
import math

import jax
import jax.numpy as jnp
from jax import lax
from jax.experimental import pallas as pl
from jax.experimental.pallas import tpu as pltpu
from jax.sharding import PartitionSpec as P

F32 = jnp.float32
BF16 = jnp.bfloat16
NN = (((1,), (0,)), ((), ()))
NT = (((1,), (1,)), ((), ()))
TN = (((0,), (0,)), ((), ()))
BLOCK = 32
TILE = 256
dot = functools.partial(lax.dot_general, preferred_element_type=F32)


def split2(x):
    high = x.astype(BF16)
    return high, (x - high.astype(F32)).astype(BF16)


def split3(x):
    high = x.astype(BF16)
    rest = x - high.astype(F32)
    middle = rest.astype(BF16)
    return high, middle, (rest - middle.astype(F32)).astype(BF16)


def left3(x):
    high, low = split2(x)
    return jnp.concatenate([high, low, high], axis=1)


def right3(x, axis=0):
    high, low = split2(x)
    return jnp.concatenate([high, high, low], axis=axis)


def eliminate(r, at):
    groups = BLOCK // 8
    rows = lax.broadcasted_iota(jnp.int32, (8, 128), 0)
    base = (at // 128) * 128
    d = r[:, base : base + 128]
    cols = []
    for q in range(BLOCK):
        lane = at - base + q
        cols.append(
            {
                g: jnp.broadcast_to(d[8 * g : 8 * g + 8, lane : lane + 1], (8, 128))
                for g in range(q // 8, groups)
            }
        )
    width = r.shape[1] // 128
    rr = [
        [r[8 * g : 8 * g + 8, 128 * c : 128 * c + 128] for c in range(width)]
        for g in range(groups)
    ]

    def spread(v, s):
        return jnp.broadcast_to(v[s : s + 1, :], (8, 128))

    for p in range(BLOCK):
        gp, sp = p // 8, p % 8
        inverse = lax.rsqrt(spread(cols[p][gp], sp))
        column = {g: cols[p][g] * inverse for g in range(gp, groups)}
        for q in range(p + 1, BLOCK):
            b = spread(column[q // 8], q % 8)
            for g in range(q // 8, groups):
                cols[q][g] = cols[q][g] - column[g] * b
        below = dict(column)
        below[gp] = jnp.where(rows > sp, column[gp], 0.0)
        for c in range(width):
            row = spread(rr[gp][c], sp) * inverse
            for g in range(gp, groups):
                new = rr[g][c] - below[g] * row
                rr[g][c] = jnp.where(rows == sp, row, new) if g == gp else new
    return jnp.concatenate([jnp.concatenate(x, axis=1) for x in rr], axis=0)


def factor_stage(k, n, m_ref, u_ref, x_ref):
    o = k * BLOCK
    e = o + BLOCK
    r = eliminate(m_ref[o:e, :], o)
    at_row = lax.broadcasted_iota(jnp.int32, (BLOCK, n), 0) + o
    at_col = lax.broadcasted_iota(jnp.int32, (BLOCK, n), 1)
    u_ref[o:e, :] = jnp.where(at_col >= at_row, r[:, :n], 0.0)
    x_ref[o:e, :] = r[:, n:]
    if e < n:
        a0 = (e // 128) * 128
        h, m, l = split3(r)
        left = jnp.concatenate([h, h, m, h, l, m], axis=0)[:, a0:n]
        right = jnp.concatenate([h, m, h, l, h, m], axis=0)
        m_ref[e:n, :] = m_ref[e:n, :] - dot(left, right, TN)[e - a0 :, :]


def exchange_kernel(
    scale, pan, tin, p3, tv, u, x, wf, pt, th, tl, ph, g1, g2, gf, m, wl, r1, r2,
    t_sem, own_sem, ps, pr, gs, grs, es, er, ws, wr,
):
    n, rows = pt.shape
    width = pan.shape[0]
    half = width // 2
    tc = tv.shape[1]
    row, col = lax.axis_index("row"), lax.axis_index("col")
    y, xx = row // 4, row % 4
    z, core = col // 2, col % 2
    up, down, far = lax.rem(z + 1, 4), lax.rem(z + 3, 4), lax.rem(z + 2, 4)
    peer_up = (row, 2 * up + core)
    peer_down = (row, 2 * down + core)
    peer_core = (row, 2 * z + 1 - core)
    place = (xx, y)

    def on_ring(axis, ahead):
        if axis == 0:
            return (4 * y + lax.rem(xx + ahead, 4), col)
        return (4 * lax.rem(y + ahead, 4) + xx, col)

    mesh = pl.DeviceIdType.MESH

    quarter = rows // 4
    loads = [
        pltpu.make_async_copy(tin.at[pl.ds(i * quarter, quarter)], tv.at[pl.ds(i * quarter, quarter)], t_sem.at[i])
        for i in range(4)
    ]
    own = pltpu.make_async_copy(pan, pt.at[pl.ds(width * col, width)], own_sem)
    own.start()
    barrier = pltpu.get_barrier_semaphore()
    around = [on_ring(axis, ahead) for axis in (0, 1) for ahead in (1, 2, 3)]
    for peer in (peer_up, peer_down, peer_core, *around):
        pl.semaphore_signal(barrier, inc=1, device_id=peer, device_id_type=mesh)
    pl.semaphore_wait(barrier, 9)

    sent = []

    def send(src, dst, ssem, rsem, peer):
        copy = pltpu.make_async_remote_copy(src, dst, ssem, rsem, device_id=peer, device_id_type=mesh)
        copy.start()
        sent.append(copy)
        return copy

    def piece(c, side):
        return pt.at[pl.ds(width * c + half * side, half)]

    def forward(index, c, side, peer):
        return send(piece(c, side), piece(c, side), ps.at[index], pr.at[index], peer)

    p0 = send(pan.at[pl.ds(0, half)], piece(col, 0), ps.at[0], pr.at[0], peer_up)
    m0 = send(pan.at[pl.ds(half, half)], piece(col, 1), ps.at[1], pr.at[1], peer_down)
    p1 = send(pan.at[pl.ds(half, half)], piece(col, 1), ps.at[2], pr.at[2], peer_up)
    m1 = send(pan.at[pl.ds(0, half)], piece(col, 0), ps.at[3], pr.at[3], peer_down)
    c0 = send(pan, pt.at[pl.ds(width * col, width)], ps.at[4], pr.at[4], peer_core)
    for load in loads:
        load.start()
    c_down, c_up, c_far = 2 * down + core, 2 * up + core, 2 * far + core

    starts = [pl.multiple_of(2 * width * q, 64) for q in (z, down, up, far)]
    tall = 2 * width

    def split_panel(b):
        at = pl.ds(starts[b], tall)
        ph[0, at], ph[1, at] = split2(pt[at])

    def product(bs, j):
        cols = slice(TILE * j, TILE * j + TILE)
        high = [ph[0, pl.ds(starts[b], tall)] for b in bs]
        low = [ph[1, pl.ds(starts[b], tall)] for b in bs]
        size = tall * len(bs)
        both = dot(jnp.concatenate(high + low, axis=0), th[:, cols], NN)
        total = both[:size] + (both[size:] + dot(jnp.concatenate(high, axis=0), tl[:, cols], NN))
        for i, b in enumerate(bs):
            wl[b, :, cols] = total[tall * i : tall * i + tall]

    short = 8
    flights = {}

    def product_send(b, phase):
        copies = []
        for h in (0, 1):
            axis = (h + phase) % 2
            first = pl.multiple_of(starts[b] + 32 * h + short * place[h], short)
            for ahead in (2, 1, 3):
                there = lax.rem(place[axis] + ahead, 4)
                if phase == 0:
                    src = wl.at[b, pl.ds(pl.multiple_of(32 * h + short * there, short), short)]
                    dst = r1.at[b, h, ahead - 1]
                elif phase == 1:
                    src = dst = r2.at[b, h, place[axis]]
                else:
                    src = dst = wf.at[pl.ds(first, short)]
                ssem, rsem = ws.at[b, phase, h, ahead - 1], wr.at[b, phase, h, ahead - 1]
                copies.append(send(src, dst, ssem, rsem, on_ring(axis, ahead)))
        flights[b, phase] = copies

    def product_step(b, phase):
        for copy in flights[b, phase]:
            copy.wait_recv()
        for h in (0, 1):
            first = pl.multiple_of(starts[b] + 32 * h + short * place[h], short)
            if phase == 0:
                mine = wl[b, pl.ds(pl.multiple_of(32 * h + short * place[h], short), short)]
                r2[b, h, place[1 - h]] = (mine + r1[b, h, 0]) + (r1[b, h, 1] + r1[b, h, 2])
            elif phase == 1:
                wf[pl.ds(first, short)] = (r2[b, h, 0] + r2[b, h, 1]) + (r2[b, h, 2] + r2[b, h, 3])
        if phase < 2:
            product_send(b, phase + 1)

    deep = n // 2
    piled = deep // 2
    half_at = pl.multiple_of(deep * core, deep)
    gram = (g1, g2)

    def gram_local():
        high, low = ph[0, pl.ds(half_at, deep)], ph[1, pl.ds(half_at, deep)]
        both = dot(jnp.concatenate([high, low], axis=0), ph[0], NT)
        total = (both[:deep] + (both[deep:] + dot(high, ph[1], NT))) * scale
        for h in (0, 1):
            g1[h, place[h]] = total[piled * h : piled * h + piled]

    def gram_send(phase):
        copies = []
        for h in (0, 1):
            axis = (h + phase) % 2
            for ahead in (2, 1, 3):
                mine = gram[phase].at[h, place[axis]]
                ssem, rsem = gs.at[phase, h, ahead - 1], grs.at[phase, h, ahead - 1]
                copies.append(send(mine, mine, ssem, rsem, on_ring(axis, ahead)))
        return copies

    def gram_add(phase, copies):
        for copy in copies:
            copy.wait_recv()
        for h in (0, 1):
            g = gram[phase]
            total = (g[h, 0] + g[h, 1]) + (g[h, 2] + g[h, 3])
            if phase == 0:
                g2[h, place[1 - h]] = total
            else:
                gf[pl.ds(pl.multiple_of(half_at + piled * h, piled), piled)] = total

    own.wait()
    c0.wait_recv()
    split_panel(0)
    p0.wait_recv()
    p2 = forward(5, c_down, 0, peer_up)
    f1 = forward(6, c_down, 0, peer_core)
    m0.wait_recv()
    m2 = forward(7, c_up, 1, peer_down)
    f2 = forward(8, c_up, 1, peer_core)
    for i in range(4):
        loads[i].wait()

        @pl.loop(0, quarter // 64)
        def _(k, i=i):
            at = pl.ds(pl.multiple_of(i * quarter + k * 64, 64), 64)
            th[at], tl[at] = split2(tv[at])

    for j in range(tc // TILE):
        product((0,), j)
    product_send(0, 0)
    p1.wait_recv()
    f3 = forward(9, c_down, 1, peer_core)
    m1.wait_recv()
    f4 = forward(10, c_up, 0, peer_core)
    for copy in (f1, f2, f3, f4):
        copy.wait_recv()
    split_panel(1)
    split_panel(2)
    for j in range(3):
        product((1, 2), j)
    p2.wait_recv()
    f5 = forward(11, c_far, 0, peer_core)
    m2.wait_recv()
    f6 = forward(12, c_far, 1, peer_core)
    product_step(0, 0)
    for j in range(3, tc // TILE):
        product((1, 2), j)
    product_send(1, 0)
    product_send(2, 0)
    f5.wait_recv()
    f6.wait_recv()
    split_panel(3)
    gram_local()
    copies = gram_send(0)
    product_step(0, 1)
    for j in range(tc // TILE):
        product((3,), j)
    product_step(1, 0)
    product_step(2, 0)
    gram_add(0, copies)
    copies = gram_send(1)
    product_send(3, 0)

    @pl.loop(0, rows // TILE)
    def _(k):
        at = pl.ds(pl.multiple_of(k * TILE, TILE), TILE)
        p3[at] = left3(pt[:, at].T)

    product_step(1, 1)
    product_step(2, 1)
    gram_add(1, copies)
    mine = gf.at[pl.ds(half_at, deep)]
    swap = send(mine, mine, es, er, peer_core)
    ri = lax.broadcasted_iota(jnp.int32, (n, n), 0)
    ci = lax.broadcasted_iota(jnp.int32, (n, n), 1)
    m[:, n:] = jnp.where(ri == ci, 1.0, 0.0).astype(F32)
    product_step(3, 0)
    swap.wait_recv()
    m[:, :n] = gf[...]

    events = [(0, 2), (3, 1), (1, 2), (2, 2), (3, 2)]
    stages = n // BLOCK
    done = 0
    for k in range(stages):
        factor_stage(k, n, m, u, x)
        goal = (len(events) * (k + 1)) // stages
        while done < goal:
            product_step(*events[done])
            done += 1
    for copy in sent:
        copy.wait_send()


def exchange(panel_t, trailing, scale):
    width, rows = panel_t.shape
    n = width * 8
    tc = trailing.shape[1]
    vm = pltpu.VMEM
    dma = pltpu.SemaphoreType.DMA
    return pl.pallas_call(
        functools.partial(exchange_kernel, scale),
        out_shape=(vm((rows, 3 * n), BF16), vm((rows, tc), F32), vm((n, n), F32), vm((n, n), F32), vm((n, tc), F32)),
        in_specs=[pl.BlockSpec(memory_space=pltpu.HBM)] * 2,
        out_specs=(pl.BlockSpec(memory_space=pltpu.VMEM),) * 5,
        scratch_shapes=[
            vm((n, rows), F32),
            vm((rows, tc), BF16),
            vm((rows, tc), BF16),
            vm((2, n, rows), BF16),
            vm((2, 4, n // 4, n), F32),
            vm((2, 4, n // 4, n), F32),
            vm((n, n), F32),
            vm((n, 2 * n), F32),
            vm((4, 2 * width, tc), F32),
            vm((4, 2, 3, 8, tc), F32),
            vm((4, 2, 4, 8, tc), F32),
            dma((4,)),
            dma,
            dma((13,)),
            dma((13,)),
            dma((2, 2, 3)),
            dma((2, 2, 3)),
            dma,
            dma,
            dma((4, 3, 2, 3)),
            dma((4, 3, 2, 3)),
        ],
        compiler_params=pltpu.CompilerParams(
            collective_id=0, has_side_effects=True, vmem_limit_bytes=36 * 2**20
        ),
        name="exchange",
    )(panel_t, trailing)


def update_kernel(inv_root, p3, tv, u, x, w, u_out, q_out, r_out, t_out, r3, x3):
    i = pl.program_id(0)
    block = q_out.shape[0]
    rows = pl.ds(pl.multiple_of(i * block, block), block)
    tiles = range(0, r_out.shape[1], TILE)

    @pl.when(i == 0)
    def _():
        x3[...] = right3(x[...].T)
        left = left3(x[...])
        for c in tiles:
            r = dot(left, right3(w[:, c : c + TILE]), NN) * inv_root
            r_out[:, c : c + TILE] = r
            r3[:, c : c + TILE] = right3(r * inv_root)
        u_out[...] = u[...]

    q = dot(p3[rows], x3[...], NN)
    q_out[...] = q
    q3 = left3(q)
    for c in tiles:
        t_out[:, c : c + TILE] = tv[rows, c : c + TILE] - dot(q3, r3[:, c : c + TILE], NN)


def update(p3, tv, u, x, w, inv_root, block=512):
    rows, tc = tv.shape
    n = u.shape[0]
    resident = pl.BlockSpec(memory_space=pltpu.VMEM)
    return pl.pallas_call(
        functools.partial(update_kernel, inv_root),
        grid=(rows // block,),
        out_shape=(
            jax.ShapeDtypeStruct((n, n), F32),
            jax.ShapeDtypeStruct((rows, n), F32),
            jax.ShapeDtypeStruct((n, tc), F32),
            jax.ShapeDtypeStruct((rows, tc), F32),
        ),
        in_specs=[resident] * 5,
        out_specs=(
            pl.BlockSpec((n, n), lambda i: (0, 0)),
            pl.BlockSpec((block, n), lambda i: (i, 0)),
            pl.BlockSpec((n, tc), lambda i: (0, 0)),
            pl.BlockSpec((block, tc), lambda i: (i, 0)),
        ),
        scratch_shapes=[pltpu.VMEM((3 * n, tc), BF16), pltpu.VMEM((3 * n, n), BF16)],
        compiler_params=pltpu.CompilerParams(vmem_limit_bytes=20 * 2**20),
        name="update",
    )(p3, tv, u, x, w)


def per_device(panel, trailing_in):
    rows_all = panel.shape[0] * lax.axis_size("row")
    p3, tv, u, x, w = exchange(panel.T, trailing_in, 1.0 / rows_all)
    return update(p3, tv, u, x, w, 1.0 / math.sqrt(rows_all))


def solution(mesh):
    in_specs = (P("row", "col"), P("row", "col"))
    out_specs = (P(), P("row", None), P(None, "col"), P("row", "col"))
    return jax.shard_map(
        per_device, mesh=mesh, in_specs=in_specs, out_specs=out_specs, check_vma=False
    )
```

```python
import functools
import math

import jax
import jax.numpy as jnp
from jax import lax
from jax.experimental import pallas as pl
from jax.experimental.pallas import tpu as pltpu
from jax.sharding import PartitionSpec as P

F32 = jnp.float32
BF16 = jnp.bfloat16
NN = (((1,), (0,)), ((), ()))
NT = (((1,), (1,)), ((), ()))
TN = (((0,), (0,)), ((), ()))
BLOCK = 32
TILE = 256
dot = functools.partial(lax.dot_general, preferred_element_type=F32)


def split2(x):
    high = x.astype(BF16)
    return high, (x - high.astype(F32)).astype(BF16)


def split3(x):
    high = x.astype(BF16)
    rest = x - high.astype(F32)
    middle = rest.astype(BF16)
    return high, middle, (rest - middle.astype(F32)).astype(BF16)


def left3(x):
    high, low = split2(x)
    return jnp.concatenate([high, low, high], axis=1)


def right3(x, axis=0):
    high, low = split2(x)
    return jnp.concatenate([high, high, low], axis=axis)


def eliminate(r, at):
    groups = BLOCK // 8
    rows = lax.broadcasted_iota(jnp.int32, (8, 128), 0)
    base = (at // 128) * 128
    d = r[:, base : base + 128]
    cols = []
    for q in range(BLOCK):
        lane = at - base + q
        cols.append(
            {
                g: jnp.broadcast_to(d[8 * g : 8 * g + 8, lane : lane + 1], (8, 128))
                for g in range(q // 8, groups)
            }
        )
    width = r.shape[1] // 128
    rr = [
        [r[8 * g : 8 * g + 8, 128 * c : 128 * c + 128] for c in range(width)]
        for g in range(groups)
    ]

    def spread(v, s):
        return jnp.broadcast_to(v[s : s + 1, :], (8, 128))

    for p in range(BLOCK):
        gp, sp = p // 8, p % 8
        inverse = lax.rsqrt(spread(cols[p][gp], sp))
        column = {g: cols[p][g] * inverse for g in range(gp, groups)}
        for q in range(p + 1, BLOCK):
            b = spread(column[q // 8], q % 8)
            for g in range(q // 8, groups):
                cols[q][g] = cols[q][g] - column[g] * b
        below = dict(column)
        below[gp] = jnp.where(rows > sp, column[gp], 0.0)
        for c in range(width):
            row = spread(rr[gp][c], sp) * inverse
            for g in range(gp, groups):
                new = rr[g][c] - below[g] * row
                rr[g][c] = jnp.where(rows == sp, row, new) if g == gp else new
    return jnp.concatenate([jnp.concatenate(x, axis=1) for x in rr], axis=0)


def factor_stage(k, n, m_ref, u_ref, x_ref):
    o = k * BLOCK
    e = o + BLOCK
    r = eliminate(m_ref[o:e, :], o)
    at_row = lax.broadcasted_iota(jnp.int32, (BLOCK, n), 0) + o
    at_col = lax.broadcasted_iota(jnp.int32, (BLOCK, n), 1)
    u_ref[o:e, :] = jnp.where(at_col >= at_row, r[:, :n], 0.0)
    x_ref[o:e, :] = r[:, n:]
    if e < n:
        a0 = (e // 128) * 128
        h, m, l = split3(r)
        left = jnp.concatenate([h, h, m, h, l, m], axis=0)[:, a0:n]
        right = jnp.concatenate([h, m, h, l, h, m], axis=0)
        m_ref[e:n, :] = m_ref[e:n, :] - dot(left, right, TN)[e - a0 :, :]


def exchange_kernel(
    scale, pan, tin, p3, tv, u, x, wf, pt, th, tl, ph, g1, g2, gf, m, wl, r1, r2,
    t_sem, own_sem, ps, pr, gs, grs, es, er, ws, wr,
):
    n, rows = pt.shape
    width = pan.shape[0]
    half = width // 2
    tc = tv.shape[1]
    row, col = lax.axis_index("row"), lax.axis_index("col")
    y, xx = row // 4, row % 4
    z, core = col // 2, col % 2
    up, down, far = lax.rem(z + 1, 4), lax.rem(z + 3, 4), lax.rem(z + 2, 4)
    peer_up = (row, 2 * up + core)
    peer_down = (row, 2 * down + core)
    peer_core = (row, 2 * z + 1 - core)
    place = (xx, y)

    def on_ring(axis, ahead):
        if axis == 0:
            return (4 * y + lax.rem(xx + ahead, 4), col)
        return (4 * lax.rem(y + ahead, 4) + xx, col)

    mesh = pl.DeviceIdType.MESH

    quarter = rows // 4
    loads = [
        pltpu.make_async_copy(tin.at[pl.ds(i * quarter, quarter)], tv.at[pl.ds(i * quarter, quarter)], t_sem.at[i])
        for i in range(4)
    ]
    own = pltpu.make_async_copy(pan, pt.at[pl.ds(width * col, width)], own_sem)
    own.start()
    barrier = pltpu.get_barrier_semaphore()
    around = [on_ring(axis, ahead) for axis in (0, 1) for ahead in (1, 2, 3)]
    for peer in (peer_up, peer_down, peer_core, *around):
        pl.semaphore_signal(barrier, inc=1, device_id=peer, device_id_type=mesh)
    pl.semaphore_wait(barrier, 9)

    sent = []

    def send(src, dst, ssem, rsem, peer):
        copy = pltpu.make_async_remote_copy(src, dst, ssem, rsem, device_id=peer, device_id_type=mesh)
        copy.start()
        sent.append(copy)
        return copy

    def piece(c, side):
        return pt.at[pl.ds(width * c + half * side, half)]

    def forward(index, c, side, peer):
        return send(piece(c, side), piece(c, side), ps.at[index], pr.at[index], peer)

    p0 = send(pan.at[pl.ds(0, half)], piece(col, 0), ps.at[0], pr.at[0], peer_up)
    m0 = send(pan.at[pl.ds(half, half)], piece(col, 1), ps.at[1], pr.at[1], peer_down)
    p1 = send(pan.at[pl.ds(half, half)], piece(col, 1), ps.at[2], pr.at[2], peer_up)
    m1 = send(pan.at[pl.ds(0, half)], piece(col, 0), ps.at[3], pr.at[3], peer_down)
    c0 = send(pan, pt.at[pl.ds(width * col, width)], ps.at[4], pr.at[4], peer_core)
    for load in loads:
        load.start()
    c_down, c_up, c_far = 2 * down + core, 2 * up + core, 2 * far + core

    starts = [pl.multiple_of(2 * width * q, 64) for q in (z, down, up, far)]
    tall = 2 * width

    def split_panel(b):
        at = pl.ds(starts[b], tall)
        ph[0, at], ph[1, at] = split2(pt[at])

    def product(bs, j):
        cols = slice(TILE * j, TILE * j + TILE)
        high = [ph[0, pl.ds(starts[b], tall)] for b in bs]
        low = [ph[1, pl.ds(starts[b], tall)] for b in bs]
        size = tall * len(bs)
        both = dot(jnp.concatenate(high + low, axis=0), th[:, cols], NN)
        total = both[:size] + (both[size:] + dot(jnp.concatenate(high, axis=0), tl[:, cols], NN))
        for i, b in enumerate(bs):
            wl[b, :, cols] = total[tall * i : tall * i + tall]

    short = 8
    flights = {}

    def product_send(b, phase):
        copies = []
        for h in (0, 1):
            axis = (h + phase) % 2
            first = pl.multiple_of(starts[b] + 32 * h + short * place[h], short)
            for ahead in (2, 1, 3):
                there = lax.rem(place[axis] + ahead, 4)
                if phase == 0:
                    src = wl.at[b, pl.ds(pl.multiple_of(32 * h + short * there, short), short)]
                    dst = r1.at[b, h, ahead - 1]
                elif phase == 1:
                    src = dst = r2.at[b, h, place[axis]]
                else:
                    src = dst = wf.at[pl.ds(first, short)]
                ssem, rsem = ws.at[b, phase, h, ahead - 1], wr.at[b, phase, h, ahead - 1]
                copies.append(send(src, dst, ssem, rsem, on_ring(axis, ahead)))
        flights[b, phase] = copies

    def product_step(b, phase):
        for copy in flights[b, phase]:
            copy.wait_recv()
        for h in (0, 1):
            first = pl.multiple_of(starts[b] + 32 * h + short * place[h], short)
            if phase == 0:
                mine = wl[b, pl.ds(pl.multiple_of(32 * h + short * place[h], short), short)]
                r2[b, h, place[1 - h]] = (mine + r1[b, h, 0]) + (r1[b, h, 1] + r1[b, h, 2])
            elif phase == 1:
                wf[pl.ds(first, short)] = (r2[b, h, 0] + r2[b, h, 1]) + (r2[b, h, 2] + r2[b, h, 3])
        if phase < 2:
            product_send(b, phase + 1)

    deep = n // 2
    piled = deep // 2
    half_at = pl.multiple_of(deep * core, deep)
    gram = (g1, g2)

    def gram_local():
        high, low = ph[0, pl.ds(half_at, deep)], ph[1, pl.ds(half_at, deep)]
        both = dot(jnp.concatenate([high, low], axis=0), ph[0], NT)
        total = (both[:deep] + (both[deep:] + dot(high, ph[1], NT))) * scale
        for h in (0, 1):
            g1[h, place[h]] = total[piled * h : piled * h + piled]

    def gram_send(phase):
        copies = []
        for h in (0, 1):
            axis = (h + phase) % 2
            for ahead in (2, 1, 3):
                mine = gram[phase].at[h, place[axis]]
                ssem, rsem = gs.at[phase, h, ahead - 1], grs.at[phase, h, ahead - 1]
                copies.append(send(mine, mine, ssem, rsem, on_ring(axis, ahead)))
        return copies

    def gram_add(phase, copies):
        for copy in copies:
            copy.wait_recv()
        for h in (0, 1):
            g = gram[phase]
            total = (g[h, 0] + g[h, 1]) + (g[h, 2] + g[h, 3])
            if phase == 0:
                g2[h, place[1 - h]] = total
            else:
                gf[pl.ds(pl.multiple_of(half_at + piled * h, piled), piled)] = total

    own.wait()
    c0.wait_recv()
    split_panel(0)
    p0.wait_recv()
    p2 = forward(5, c_down, 0, peer_up)
    f1 = forward(6, c_down, 0, peer_core)
    m0.wait_recv()
    m2 = forward(7, c_up, 1, peer_down)
    f2 = forward(8, c_up, 1, peer_core)
    for i in range(4):
        loads[i].wait()

        @pl.loop(0, quarter // 64)
        def _(k, i=i):
            at = pl.ds(pl.multiple_of(i * quarter + k * 64, 64), 64)
            th[at], tl[at] = split2(tv[at])

    for j in range(tc // TILE):
        product((0,), j)
    product_send(0, 0)
    p1.wait_recv()
    f3 = forward(9, c_down, 1, peer_core)
    m1.wait_recv()
    f4 = forward(10, c_up, 0, peer_core)
    for copy in (f1, f2, f3, f4):
        copy.wait_recv()
    split_panel(1)
    split_panel(2)
    for j in range(3):
        product((1, 2), j)
    p2.wait_recv()
    f5 = forward(11, c_far, 0, peer_core)
    m2.wait_recv()
    f6 = forward(12, c_far, 1, peer_core)
    product_step(0, 0)
    for j in range(3, tc // TILE):
        product((1, 2), j)
    product_send(1, 0)
    product_send(2, 0)
    f5.wait_recv()
    f6.wait_recv()
    split_panel(3)
    gram_local()
    copies = gram_send(0)
    product_step(0, 1)
    for j in range(tc // TILE):
        product((3,), j)
    product_step(1, 0)
    product_step(2, 0)
    gram_add(0, copies)
    copies = gram_send(1)
    product_send(3, 0)

    @pl.loop(0, rows // TILE)
    def _(k):
        at = pl.ds(pl.multiple_of(k * TILE, TILE), TILE)
        p3[at] = left3(pt[:, at].T)

    product_step(1, 1)
    product_step(2, 1)
    gram_add(1, copies)
    mine = gf.at[pl.ds(half_at, deep)]
    swap = send(mine, mine, es, er, peer_core)
    ri = lax.broadcasted_iota(jnp.int32, (n, n), 0)
    ci = lax.broadcasted_iota(jnp.int32, (n, n), 1)
    m[:, n:] = jnp.where(ri == ci, 1.0, 0.0).astype(F32)
    product_step(3, 0)
    swap.wait_recv()
    m[:, :n] = gf[...]

    events = [(0, 2), (3, 1), (1, 2), (2, 2), (3, 2)]
    stages = n // BLOCK
    done = 0
    for k in range(stages):
        factor_stage(k, n, m, u, x)
        goal = (len(events) * (k + 1)) // stages
        while done < goal:
            product_step(*events[done])
            done += 1
    for copy in sent:
        copy.wait_send()


def exchange(panel_t, trailing, scale):
    width, rows = panel_t.shape
    n = width * 8
    tc = trailing.shape[1]
    vm = pltpu.VMEM
    dma = pltpu.SemaphoreType.DMA
    return pl.pallas_call(
        functools.partial(exchange_kernel, scale),
        out_shape=(vm((rows, 3 * n), BF16), vm((rows, tc), F32), vm((n, n), F32), vm((n, n), F32), vm((n, tc), F32)),
        in_specs=[pl.BlockSpec(memory_space=pltpu.HBM)] * 2,
        out_specs=(pl.BlockSpec(memory_space=pltpu.VMEM),) * 5,
        scratch_shapes=[
            vm((n, rows), F32),
            vm((rows, tc), BF16),
            vm((rows, tc), BF16),
            vm((2, n, rows), BF16),
            vm((2, 4, n // 4, n), F32),
            vm((2, 4, n // 4, n), F32),
            vm((n, n), F32),
            vm((n, 2 * n), F32),
            vm((4, 2 * width, tc), F32),
            vm((4, 2, 3, 8, tc), F32),
            vm((4, 2, 4, 8, tc), F32),
            dma((4,)),
            dma,
            dma((13,)),
            dma((13,)),
            dma((2, 2, 3)),
            dma((2, 2, 3)),
            dma,
            dma,
            dma((4, 3, 2, 3)),
            dma((4, 3, 2, 3)),
        ],
        compiler_params=pltpu.CompilerParams(
            collective_id=0, has_side_effects=True, vmem_limit_bytes=36 * 2**20
        ),
        name="exchange",
    )(panel_t, trailing)


def update_kernel(inv_root, p3, tv, u, x, w, u_out, q_out, r_out, t_out, r3, x3):
    i = pl.program_id(0)
    block = q_out.shape[0]
    rows = pl.ds(pl.multiple_of(i * block, block), block)
    tiles = range(0, r_out.shape[1], TILE)

    @pl.when(i == 0)
    def _():
        x3[...] = right3(x[...].T)
        left = left3(x[...])
        for c in tiles:
            r = dot(left, right3(w[:, c : c + TILE]), NN) * inv_root
            r_out[:, c : c + TILE] = r
            r3[:, c : c + TILE] = right3(r * inv_root)
        u_out[...] = u[...]

    q = dot(p3[rows], x3[...], NN)
    q_out[...] = q
    q3 = left3(q)
    for c in tiles:
        t_out[:, c : c + TILE] = tv[rows, c : c + TILE] - dot(q3, r3[:, c : c + TILE], NN)


def update(p3, tv, u, x, w, inv_root, block=512):
    rows, tc = tv.shape
    n = u.shape[0]
    resident = pl.BlockSpec(memory_space=pltpu.VMEM)
    return pl.pallas_call(
        functools.partial(update_kernel, inv_root),
        grid=(rows // block,),
        out_shape=(
            jax.ShapeDtypeStruct((n, n), F32),
            jax.ShapeDtypeStruct((rows, n), F32),
            jax.ShapeDtypeStruct((n, tc), F32),
            jax.ShapeDtypeStruct((rows, tc), F32),
        ),
        in_specs=[resident] * 5,
        out_specs=(
            pl.BlockSpec((n, n), lambda i: (0, 0)),
            pl.BlockSpec((block, n), lambda i: (i, 0)),
            pl.BlockSpec((n, tc), lambda i: (0, 0)),
            pl.BlockSpec((block, tc), lambda i: (i, 0)),
        ),
        scratch_shapes=[pltpu.VMEM((3 * n, tc), BF16), pltpu.VMEM((3 * n, n), BF16)],
        compiler_params=pltpu.CompilerParams(vmem_limit_bytes=20 * 2**20),
        name="update",
    )(p3, tv, u, x, w)


def per_device(panel, trailing_in):
    rows_all = panel.shape[0] * lax.axis_size("row")
    p3, tv, u, x, w = exchange(pltpu.with_memory_space_constraint(panel.T, pltpu.HBM), trailing_in, 1.0 / rows_all)
    return update(p3, tv, u, x, w, 1.0 / math.sqrt(rows_all))


def solution(mesh):
    in_specs = (P("row", "col"), P("row", "col"))
    out_specs = (P(), P("row", None), P(None, "col"), P("row", "col"))
    return jax.shard_map(
        per_device, mesh=mesh, in_specs=in_specs, out_specs=out_specs, check_vma=False
    )
```
